32 devices in a mesh: dp: 2 (over x), expert: 16 (over z, y, core).
Axes of the slice: x: 2, y: 2, z: 4, core: 2. Of those that a mesh axis runs over, the one named last changes fastest.
Arguments:
- tokens: bfloat16 [1024, 4096], P(('dp', 'expert')), may hold values from -6 to 6
- out_grad: bfloat16 [1024, 4096], P(('dp', 'expert')), may hold values from -24 to 24
- routes: int32 [1024, 8], P(('dp', 'expert')), may hold values from 0 to 15, all different within a row; in each aligned block of 32 rows (0 to 31, 32 to 63, ...) at most 18 rows name the same one
- probs: bfloat16 [1024, 8], P(('dp', 'expert')), may hold values from 0.049804688 to 0.29882812
- w_gate: bfloat16 [16, 4096, 1536], P('expert', None, 'dp'), may hold values from -0.09375 to 0.09375
- w_up: bfloat16 [16, 4096, 1536], P('expert', None, 'dp'), may hold values from -0.09375 to 0.09375
- w_down: bfloat16 [16, 1536, 4096], P('expert', 'dp'), may hold values from -0.15625 to 0.15625
Outputs:
- mixed: bfloat16 [1024, 4096], P(('dp', 'expert'))
- input_factor: float32 [16, 1536, 1536], P('expert', 'dp')
- output_factor: bfloat16 [16, 4096, 4096], P('expert', 'dp')
The draws below stay inside these ranges and needn't reach their ends.
Inputs may be any that keep to these rules, and one draw needn't show every extreme that they name: `routes`: each token names 8 different experts. Among the 32 tokens of one device no expert is named more than 18 times, and in some device's tokens an expert is named exactly 18 times.
All inputs are finite; a program needn't handle non-finite values.
Results may differ from the reference program's by a relative error of at most 0.015.
Values may be sent and summed in bfloat16 or wider, within the bound.
A program may use at most 192 MiB of HBM per device.

```python
import math
import jax
import jax.numpy as jnp
import numpy as np
from jax import lax

D = 4096
F = 1536
TOPK = 8
TOK_DEV = 32
EXPERTS = 16
CAP = 18
TOKENS = 1024
ROUTED = 512
N_DP = 2


def block_levels(own_key, shape, pieces, low, high):
    gain, own = 1.0, jax.random.fold_in(own_key, 6)
    for axis_at, blocks in pieces:
        steps = jnp.exp(jax.random.uniform(jax.random.fold_in(own, axis_at), (blocks,), jnp.float32, low / len(pieces), high / len(pieces)))
        gain = gain * jnp.repeat(steps, shape[axis_at] // blocks).reshape([-1 if axis == axis_at else 1 for axis in range(len(shape))])
    return gain


def assign_block(key, own, number, rows, number_of, top, most, skew):
    sequence = jax.random.permutation(key, number_of)
    crowded, common = shares(number_of, rows * top, most, skew, True), shares(number_of, rows * top, most, skew, False)
    places = jnp.arange(number_of)

    def named(tallies, turn):
        used = int((tallies > 0).sum())
        fixed = max(1, used // 4)
        shifted = fixed + (places - fixed + turn * (used - fixed)) % max(1, number_of - fixed)
        return jnp.zeros((number_of,), jnp.int32).at[sequence[jnp.where(places < fixed, places, shifted)]].set(jnp.asarray(tallies, jnp.int32))

    tallies = jnp.where(number % 4 == 0, named(crowded, number // 4), named(common, number - number // 4 - 1))
    mixed = jax.random.permutation(jax.random.fold_in(own, 3), number_of)
    source_of, receiver = mixed[0:number_of // 2 * 2:2], mixed[1:number_of // 2 * 2:2]
    margin = jnp.minimum(tallies[source_of] - 1, most - tallies[receiver]) // 2
    margin = jnp.where((source_of == sequence[0]) | (receiver == sequence[0]) | (tallies[receiver] == 0), 0, jnp.maximum(margin, 0))
    shifted = jax.random.randint(jax.random.fold_in(own, 4), (number_of // 2,), 0, 1 << 20) % (margin + 1)
    tallies = tallies.at[source_of].add(-shifted).at[receiver].add(shifted)
    members = jnp.searchsorted(jnp.cumsum(tallies), jnp.arange(rows * top), side="right").astype(jnp.int32)
    grid = members.reshape(top, rows).T
    grid = grid[jax.random.permutation(jax.random.fold_in(own, 1), rows)]
    turn = jax.random.randint(jax.random.fold_in(own, 2), (rows, 1), 0, top)
    return jnp.take_along_axis(grid, (jnp.arange(top)[None, :] + turn) % top, axis=1)


def shares(amount, total, most, lean, full):
    weights = [(1 << 20) // math.isqrt(grade ** lean) + 1 for grade in range(1, amount + 1)]
    largest = most if full else min(most, max(-(-total // amount), total * weights[0] // sum(weights)))
    least = 1 if total - largest >= amount - 1 else 0
    given, rest = [largest] + [least] * (amount - 1), total - largest - least * (amount - 1)
    while rest > 0:
        movable = [i for i in range(1, amount) if given[i] < largest] or [i for i in range(1, amount) if given[i] < most]
        pool, budget = sum([weights[i] for i in movable]), rest
        for i in movable:
            extra = min(most - given[i], max(1, budget * weights[i] // pool), rest)
            given[i] = given[i] + extra
            rest = rest - extra
    return np.array(given)


def normal_values(stream_key, shape, width, most, pieces=(), kind=jnp.bfloat16):
    result = width * jax.random.normal(stream_key, shape, jnp.float32)
    if pieces:
        result = result * block_levels(stream_key, shape, pieces, -0.22, 0.18)
    return jnp.clip(result, -most, most).astype(kind)


def setup_inputs(seed: int = 0) -> dict:
    streams_of = jax.random.split(jax.random.key(seed), 8)
    tokens = normal_values(streams_of[0], (TOKENS, D), 1.0, 6.0, ((0, 32),))
    out_grad = normal_values(streams_of[1], (TOKENS, D), 4.0, 24.0, ((0, 32),))
    routes_keys = jax.random.split(jax.random.fold_in(streams_of[2], 1), TOKENS // TOK_DEV)
    routes_turns = jax.random.permutation(jax.random.fold_in(streams_of[2], 3), TOKENS // TOK_DEV)
    routes = jax.vmap(lambda own, number: assign_block(jax.random.fold_in(streams_of[2], 2), own, number, TOK_DEV, EXPERTS, TOPK, CAP, 1))(routes_keys, routes_turns).reshape((TOKENS, TOPK))
    probs = jnp.clip(0.049804688 + 0.24902344 * jax.random.uniform(streams_of[3], (TOKENS, TOPK), jnp.float32) ** block_levels(streams_of[3], (TOKENS, TOPK), ((0, 32),), -0.2, 0.2), 0.049804688, 0.29882812).astype(jnp.bfloat16)
    w_gate = normal_values(streams_of[4], (EXPERTS, D, F), D ** -0.5, 0.09375, ((0, 16), (2, 2)))
    w_up = normal_values(streams_of[5], (EXPERTS, D, F), D ** -0.5, 0.09375, ((0, 16), (2, 2)))
    w_down = normal_values(streams_of[6], (EXPERTS, F, D), F ** -0.5, 0.15625, ((0, 16), (1, 2)))
    return {"tokens": tokens, "out_grad": out_grad, "routes": routes, "probs": probs, "w_gate": w_gate, "w_up": w_up, "w_down": w_down}


def slot_positions(routes):
    blocks = routes.reshape(-1, TOK_DEV * TOPK)
    onehot = (blocks[:, :, None] == jnp.arange(EXPERTS, dtype=jnp.int32)[None, None, :]).astype(jnp.int32)
    earlier = jnp.cumsum(onehot, axis=1) - onehot
    return jnp.sum(earlier * onehot, axis=2).reshape(TOKENS, TOPK).astype(jnp.int32)


def reference(tokens, out_grad, routes, probs, w_gate, w_up, w_down):
    slot_index = slot_positions(routes)
    token_ids = jnp.broadcast_to(jnp.arange(TOKENS, dtype=jnp.int32)[:, None], (TOKENS, TOPK))
    place = ((token_ids // TOK_DEV) * CAP + slot_index).astype(jnp.int32)
    buffer_rows = (TOKENS // TOK_DEV) * CAP
    table = jnp.full((EXPERTS, buffer_rows), TOKENS, dtype=jnp.int32).at[routes, place].set(token_ids)
    prob_table = jnp.zeros((EXPERTS, buffer_rows), jnp.float32).at[routes, place].set(probs.astype(jnp.float32))
    padded_x = jnp.concatenate([tokens, jnp.zeros((1, D), tokens.dtype)], 0)
    padded_g = jnp.concatenate([out_grad, jnp.zeros((1, D), out_grad.dtype)], 0)
    piece_width = F // N_DP

    def one_expert(index):
        row_ids = table[index]
        rows_x = padded_x[row_ids]
        gate = jnp.dot(rows_x, w_gate[index], preferred_element_type=jnp.float32)
        upward = jnp.dot(rows_x, w_up[index], preferred_element_type=jnp.float32)
        hidden = (jax.nn.silu(gate) * upward).astype(jnp.bfloat16)
        down_matrix = w_down[index]
        summed = jnp.zeros((buffer_rows, D), jnp.float32)
        for share in range(N_DP):
            term = jnp.dot(hidden[:, share * piece_width:(share + 1) * piece_width],
                           down_matrix[share * piece_width:(share + 1) * piece_width],
                           preferred_element_type=jnp.float32)
            rounded = lax.optimization_barrier(term.astype(jnp.bfloat16))
            summed = summed + rounded.astype(jnp.float32)
        expert_out = summed.astype(jnp.bfloat16)
        input_factor = jnp.dot(hidden.T, hidden, preferred_element_type=jnp.float32) / ROUTED
        grad_rows = (prob_table[index][:, None] * padded_g[row_ids].astype(jnp.float32)).astype(jnp.bfloat16)
        output_factor = (jnp.dot(grad_rows.T, grad_rows, preferred_element_type=jnp.float32) / ROUTED).astype(jnp.bfloat16)
        return expert_out, input_factor, output_factor

    expert_outs, input_factor, output_factor = lax.map(one_expert, jnp.arange(EXPERTS, dtype=jnp.int32))
    picked = expert_outs[routes, place]
    mixed = jnp.einsum("tk,tkd->td", probs.astype(jnp.float32), picked.astype(jnp.float32)).astype(jnp.bfloat16)
    return mixed, input_factor, output_factor
```

```python
import jax
import jax.numpy as jnp
from jax import lax
from jax.experimental import pallas as pl
from jax.experimental.pallas import tpu as pltpu
from jax.sharding import PartitionSpec as P

AXES = ("dp", "expert")
MESH = pl.DeviceIdType.MESH
STRIP = 512


def gram(left, right):
    return lax.dot_general(
        left, right, (((0,), (0,)), ((), ())), preferred_element_type=jnp.float32
    )


class Place:
    def __init__(self):
        self.dp = lax.axis_index("dp")
        expert = lax.axis_index("expert")
        self.z = expert // 4
        self.y = (expert // 2) % 2
        self.c = expert % 2

    def far(self, step):
        return lax.rem(self.z + step, 4)

    def flipped(self, first, second):
        over_dp = first * (1 - self.c) + second * self.c
        over_y = first * self.c + second * (1 - self.c)
        return (
            self.dp + over_dp * (1 - 2 * self.dp),
            self.y + over_y * (1 - 2 * self.y),
        )

    def device(self, first=0, second=0, step=0, sibling=0):
        dp, y = self.flipped(first, second)
        return (dp, self.far(step) * 4 + y * 2 + self.core(sibling))

    def core(self, sibling):
        return self.c + sibling * (1 - 2 * self.c)

    def block(self, first=0, second=0, step=0, sibling=0):
        dp, expert = self.device(first, second, step, sibling)
        return dp * 16 + expert

    def greet(self):
        barrier = pltpu.get_barrier_semaphore()
        peers = [self.device(step=step) for step in (1, 2, 3)]
        peers += [self.device(first=1), self.device(second=1), self.device(sibling=1)]
        for peer in peers:
            pl.semaphore_signal(barrier, inc=1, device_id=peer, device_id_type=MESH)
        pl.semaphore_wait(barrier, len(peers))


def rows_of(ref, block):
    return ref.at[pl.ds(pl.multiple_of(block * 32, 32), 32)]


def gather_kernel(count, *refs):
    ins, outs = refs[:count], refs[count : 2 * count]
    local_sem, z_sem, first_sem, second_sem, sibling_sem, recv_sem = refs[2 * count :]
    at = Place()
    at.greet()
    started = []

    def send(a, block, sem, peer, src=None):
        copy = pltpu.make_async_remote_copy(
            src_ref=rows_of(outs[a], block) if src is None else src,
            dst_ref=rows_of(outs[a], block),
            send_sem=sem,
            recv_sem=recv_sem.at[a, block],
            device_id=peer,
            device_id_type=MESH,
        )
        copy.start()
        started.append(copy)

    def arrived(a, block):
        pltpu.make_async_remote_copy(
            src_ref=rows_of(outs[a], block),
            dst_ref=rows_of(outs[a], block),
            send_sem=local_sem.at[a],
            recv_sem=recv_sem.at[a, block],
            device_id=at.device(sibling=1),
            device_id_type=MESH,
        ).wait_recv()

    def forward(a, first, second, step, own=False):
        block = at.block(first, second, step)
        src = None
        if own:
            src = ins[a]
        else:
            arrived(a, block)
        if not second:
            if not first:
                send(a, block, first_sem.at[a, step], at.device(first=1), src)
            send(a, block, second_sem.at[a, 4 * first + step], at.device(second=1), src)
        send(a, block, sibling_sem.at[a, 8 * first + 4 * second + step], at.device(sibling=1), src)

    for a in range(count):
        for step in (2, 1, 3):
            send(a, at.block(), z_sem.at[a, step], at.device(step=step), ins[a])
    local = []
    for a in range(count):
        forward(a, 0, 0, 0, own=True)
        local.append(pltpu.make_async_copy(ins[a], rows_of(outs[a], at.block()), local_sem.at[a]))
        local[-1].start()
    near, mid, far = ([], [], [])
    for step in (0, 1, 3, 2):
        if step:
            near.append((0, 0, step))
        mid.append((1, 0, step))
        far += [(0, 1, step), (1, 1, step)]
    for turn in range(count + 2):
        for a in range(count):
            stage = turn - a
            for hop in (near, mid, far)[stage] if 0 <= stage < 3 else ():
                forward(a, *hop)
    for copy in local:
        copy.wait()
    for copy in started:
        copy.wait_send()
    for a in range(count):
        for first in range(2):
            for second in range(2):
                for step in range(4):
                    arrived(a, at.block(first, second, step, sibling=1))


def gather_rows(*arrays):
    count = len(arrays)
    anywhere = pl.BlockSpec(memory_space=pl.ANY)
    dma = pltpu.SemaphoreType.DMA
    return pl.pallas_call(
        lambda *refs: gather_kernel(count, *refs),
        out_shape=[
            jax.ShapeDtypeStruct((32 * array.shape[0], array.shape[1]), array.dtype)
            for array in arrays
        ],
        in_specs=[anywhere] * count,
        out_specs=[anywhere] * count,
        scratch_shapes=[
            dma((count,)),
            dma((count, 4)),
            dma((count, 4)),
            dma((count, 8)),
            dma((count, 16)),
            dma((count, 32)),
        ],
        compiler_params=pltpu.CompilerParams(collective_id=0, has_side_effects=True),
        name="gather_rows",
    )(*arrays)


def scatter_kernel(share, out, held0, held1, held2, held3, sent, s0, s1, s2, s3, r0, r1, r2, r3):
    at = Place()
    at.greet()
    started = []

    def copy_of(src, dst, send_sem, recv_sem, peer):
        return pltpu.make_async_remote_copy(
            src_ref=src,
            dst_ref=dst,
            send_sem=send_sem,
            recv_sem=recv_sem,
            device_id=peer,
            device_id_type=MESH,
        )

    def send(*args):
        copy = copy_of(*args)
        copy.start()
        started.append(copy)

    def arrived(dst, recv_sem):
        copy_of(dst, dst, s0.at[0], recv_sem, at.device(sibling=1)).wait_recv()

    def slot(first, second, step):
        dp, y = at.flipped(first, second)
        return dp * 8 + at.far(step) * 2 + y

    def add(dst, terms):
        def strip(i, carry):
            columns = pl.ds(pl.multiple_of(i * STRIP, STRIP), STRIP)
            total = terms[0][:, columns].astype(jnp.float32)
            for term in terms[1:]:
                total = total + term[:, columns].astype(jnp.float32)
            dst[:, columns] = total.astype(dst.dtype)
            return carry

        lax.fori_loop(0, out.shape[1] // STRIP, strip, 0)

    def both_cores(first, second, step):
        place = slot(first, second, step)
        arrived(held0.at[place], r0.at[place])
        return [rows_of(share, at.block(first, second, step)), held0.at[place]]

    def stage_a(step):
        for first in range(2):
            mine = sent.at[4 * first + step]
            add(mine, both_cores(first, 1, step))
            place = 4 * first + step
            send(mine, held1.at[place], s1.at[place], r1.at[place], at.device(second=1))

    def stage_b(step):
        mine = sent.at[8 + step]
        arrived(held1.at[4 + step], r1.at[4 + step])
        add(mine, both_cores(1, 0, step) + [held1.at[4 + step]])
        send(mine, held2.at[step], s2.at[step], r2.at[step], at.device(first=1))

    def stage_c(step):
        arrived(held1.at[step], r1.at[step])
        arrived(held2.at[step], r2.at[step])
        terms = both_cores(0, 0, step) + [held1.at[step], held2.at[step]]
        if step:
            mine = sent.at[12 + step]
            add(mine, terms)
            send(mine, held3.at[step], s3.at[step], r3.at[step], at.device(step=step))
        else:
            for other in (1, 3, 2):
                arrived(held3.at[other], r3.at[other])
                terms.append(held3.at[other])
            add(out, terms)

    order = (2, 1, 3, 0)
    for step in order:
        for second in (1, 0):
            for first in (1, 0):
                place = slot(first, second, step)
                send(
                    rows_of(share, at.block(first, second, step, sibling=1)),
                    held0.at[place],
                    s0.at[place],
                    r0.at[place],
                    at.device(sibling=1),
                )
    for turn in range(6):
        if turn < 4:
            stage_a(order[turn])
        if 1 <= turn < 5:
            stage_b(order[turn - 1])
        if 2 <= turn:
            stage_c(order[turn - 2])
    for copy in started:
        copy.wait_send()


def scatter_rows(share):
    width = share.shape[1]
    held = lambda count: pltpu.VMEM((count, 32, width), share.dtype)
    dma = pltpu.SemaphoreType.DMA
    whole = pl.BlockSpec(memory_space=pltpu.VMEM)
    return pl.pallas_call(
        scatter_kernel,
        out_shape=jax.ShapeDtypeStruct((32, width), share.dtype),
        in_specs=[whole],
        out_specs=whole,
        scratch_shapes=[held(16), held(8), held(4), held(4), held(16)]
        + [dma((count,)) for count in (16, 8, 4, 4) * 2],
        compiler_params=pltpu.CompilerParams(
            collective_id=1, has_side_effects=True, vmem_limit_bytes=40 * 1024 * 1024
        ),
        name="scatter_rows",
    )(share)


def on_device(tokens, out_grad, routes, probs, w_gate, w_up, w_down):
    n_data = lax.axis_size("dp")
    n_owner = lax.axis_size("expert")
    tok_count, top_count = routes.shape
    width = tokens.shape[1]
    routed = tok_count * top_count * n_data
    here = lax.axis_index("dp")
    expert = lax.axis_index("expert")
    torus = n_data == 2 and n_owner == 16 and tok_count == 32
    ids = jnp.arange(128 if torus else n_owner, dtype=jnp.int32)
    table = jnp.sum(
        jnp.where(routes[:, :, None] == ids, probs.astype(jnp.float32)[:, :, None], 0.0), axis=1
    ).astype(jnp.bfloat16)
    if torus:
        all_table, all_x, all_g = gather_rows(table, tokens, out_grad)
    else:
        all_table = lax.all_gather(table, AXES, axis=0, tiled=True)
        all_x = lax.all_gather(tokens, AXES, axis=0, tiled=True)
        all_g = lax.all_gather(out_grad, AXES, axis=0, tiled=True)
    weight = jnp.sum(
        jnp.where(ids[None, :] == expert, all_table.astype(jnp.float32), 0.0), axis=1
    )[:, None]
    gate = jnp.dot(all_x, w_gate[0], preferred_element_type=jnp.float32)
    upward = jnp.dot(all_x, w_up[0], preferred_element_type=jnp.float32)
    hidden = jnp.where(weight > 0, jax.nn.silu(gate) * upward, 0.0).astype(jnp.bfloat16)
    other_hidden = lax.all_gather(hidden, "dp", axis=1, tiled=True)
    share = weight * jnp.dot(hidden, w_down[0], preferred_element_type=jnp.float32)
    share = share.astype(jnp.bfloat16)
    if torus:
        mixed = scatter_rows(share)
    else:
        mixed = lax.psum_scatter(share, AXES, scatter_dimension=0, tiled=True)
    input_factor = (gram(hidden, other_hidden) / routed)[None]
    grad_rows = (weight * all_g.astype(jnp.float32)).astype(jnp.bfloat16)
    slice_width = width // n_data
    own_cols = lax.dynamic_slice_in_dim(grad_rows, here * slice_width, slice_width, 1)
    output_factor = (gram(own_cols, grad_rows) / routed).astype(jnp.bfloat16)[None]
    return (mixed, input_factor, output_factor)


def solution(mesh):
    rows = P(AXES, None)
    in_specs = (
        rows,
        rows,
        rows,
        rows,
        P("expert", None, "dp"),
        P("expert", None, "dp"),
        P("expert", "dp", None),
    )
    out_specs = (rows, P("expert", "dp", None), P("expert", "dp", None))
    return jax.shard_map(
        on_device, mesh=mesh, in_specs=in_specs, out_specs=out_specs, check_vma=False
    )
```

```python
import jax
import jax.numpy as jnp
from jax import lax
from jax.experimental import pallas as pl
from jax.experimental.pallas import tpu as pltpu
from jax.sharding import PartitionSpec as P

AXES = ("dp", "expert")
MESH = pl.DeviceIdType.MESH
STRIP = 512


def gram(left, right):
    return lax.dot_general(
        left, right, (((0,), (0,)), ((), ())), preferred_element_type=jnp.float32
    )


class Place:
    def __init__(self):
        self.dp = lax.axis_index("dp")
        expert = lax.axis_index("expert")
        self.z = expert // 4
        self.y = (expert // 2) % 2
        self.c = expert % 2

    def far(self, step):
        return lax.rem(self.z + step, 4)

    def flipped(self, first, second):
        over_dp = first * (1 - self.c) + second * self.c
        over_y = first * self.c + second * (1 - self.c)
        return (
            self.dp + over_dp * (1 - 2 * self.dp),
            self.y + over_y * (1 - 2 * self.y),
        )

    def device(self, first=0, second=0, step=0, sibling=0):
        dp, y = self.flipped(first, second)
        return (dp, self.far(step) * 4 + y * 2 + self.core(sibling))

    def core(self, sibling):
        return self.c + sibling * (1 - 2 * self.c)

    def block(self, first=0, second=0, step=0, sibling=0):
        dp, expert = self.device(first, second, step, sibling)
        return dp * 16 + expert

    def greet(self):
        barrier = pltpu.get_barrier_semaphore()
        peers = [self.device(step=step) for step in (1, 2, 3)]
        peers += [self.device(first=1), self.device(second=1), self.device(sibling=1)]
        for peer in peers:
            pl.semaphore_signal(barrier, inc=1, device_id=peer, device_id_type=MESH)
        pl.semaphore_wait(barrier, len(peers))


def rows_of(ref, block):
    return ref.at[pl.ds(pl.multiple_of(block * 32, 32), 32)]


def gather_kernel(count, *refs):
    ins, outs = refs[:count], refs[count : 2 * count]
    local_sem, z_sem, first_sem, second_sem, sibling_sem, recv_sem = refs[2 * count :]
    at = Place()
    at.greet()
    started = []

    def send(a, block, sem, peer, src=None):
        copy = pltpu.make_async_remote_copy(
            src_ref=rows_of(outs[a], block) if src is None else src,
            dst_ref=rows_of(outs[a], block),
            send_sem=sem,
            recv_sem=recv_sem.at[a, block],
            device_id=peer,
            device_id_type=MESH,
        )
        copy.start()
        started.append(copy)

    def arrived(a, block):
        pltpu.make_async_remote_copy(
            src_ref=rows_of(outs[a], block),
            dst_ref=rows_of(outs[a], block),
            send_sem=local_sem.at[a],
            recv_sem=recv_sem.at[a, block],
            device_id=at.device(sibling=1),
            device_id_type=MESH,
        ).wait_recv()

    def forward(a, first, second, step, own=False):
        block = at.block(first, second, step)
        src = None
        if own:
            src = ins[a]
        else:
            arrived(a, block)
        if not second:
            if not first:
                send(a, block, first_sem.at[a, step], at.device(first=1), src)
            send(a, block, second_sem.at[a, 4 * first + step], at.device(second=1), src)
        send(a, block, sibling_sem.at[a, 8 * first + 4 * second + step], at.device(sibling=1), src)

    for a in range(count):
        for step in (2, 1, 3):
            send(a, at.block(), z_sem.at[a, step], at.device(step=step), ins[a])
    local = []
    for a in range(count):
        forward(a, 0, 0, 0, own=True)
        local.append(pltpu.make_async_copy(ins[a], rows_of(outs[a], at.block()), local_sem.at[a]))
        local[-1].start()
    near, mid, far = ([], [], [])
    for step in (0, 1, 3, 2):
        if step:
            near.append((0, 0, step))
        mid.append((1, 0, step))
        far += [(0, 1, step), (1, 1, step)]
    for turn in range(count + 2):
        for a in range(count):
            stage = turn - a
            for hop in (near, mid, far)[stage] if 0 <= stage < 3 else ():
                forward(a, *hop)
    for copy in local:
        copy.wait()
    for copy in started:
        copy.wait_send()
    for a in range(count):
        for first in range(2):
            for second in range(2):
                for step in range(4):
                    arrived(a, at.block(first, second, step, sibling=1))


def gather_rows(*arrays):
    count = len(arrays)
    anywhere = pl.BlockSpec(memory_space=pl.ANY)
    dma = pltpu.SemaphoreType.DMA
    return pl.pallas_call(
        lambda *refs: gather_kernel(count, *refs),
        out_shape=[
            jax.ShapeDtypeStruct((32 * array.shape[0], array.shape[1]), array.dtype)
            for array in arrays
        ],
        in_specs=[anywhere] * count,
        out_specs=[anywhere] * count,
        scratch_shapes=[
            dma((count,)),
            dma((count, 4)),
            dma((count, 4)),
            dma((count, 8)),
            dma((count, 16)),
            dma((count, 32)),
        ],
        compiler_params=pltpu.CompilerParams(collective_id=0, has_side_effects=True),
        name="gather_rows",
    )(*arrays)


def scatter_kernel(share, out, held0, held1, held2, held3, sent, s0, s1, s2, s3, r0, r1, r2, r3):
    at = Place()
    at.greet()
    started = []

    def copy_of(src, dst, send_sem, recv_sem, peer):
        return pltpu.make_async_remote_copy(
            src_ref=src,
            dst_ref=dst,
            send_sem=send_sem,
            recv_sem=recv_sem,
            device_id=peer,
            device_id_type=MESH,
        )

    def send(*args):
        copy = copy_of(*args)
        copy.start()
        started.append(copy)

    def arrived(dst, recv_sem):
        copy_of(dst, dst, s0.at[0], recv_sem, at.device(sibling=1)).wait_recv()

    def slot(first, second, step):
        dp, y = at.flipped(first, second)
        return dp * 8 + at.far(step) * 2 + y

    def add(dst, terms):
        def strip(i, carry):
            columns = pl.ds(pl.multiple_of(i * STRIP, STRIP), STRIP)
            total = terms[0][:, columns].astype(jnp.float32)
            for term in terms[1:]:
                total = total + term[:, columns].astype(jnp.float32)
            dst[:, columns] = total.astype(dst.dtype)
            return carry

        lax.fori_loop(0, out.shape[1] // STRIP, strip, 0)

    def both_cores(first, second, step):
        place = slot(first, second, step)
        arrived(held0.at[place], r0.at[place])
        return [rows_of(share, at.block(first, second, step)), held0.at[place]]

    def stage_a(step):
        for first in range(2):
            mine = sent.at[4 * first + step]
            add(mine, both_cores(first, 1, step))
            place = 4 * first + step
            send(mine, held1.at[place], s1.at[place], r1.at[place], at.device(second=1))

    def stage_b(step):
        mine = sent.at[8 + step]
        arrived(held1.at[4 + step], r1.at[4 + step])
        add(mine, both_cores(1, 0, step) + [held1.at[4 + step]])
        send(mine, held2.at[step], s2.at[step], r2.at[step], at.device(first=1))

    def stage_c(step):
        arrived(held1.at[step], r1.at[step])
        arrived(held2.at[step], r2.at[step])
        terms = both_cores(0, 0, step) + [held1.at[step], held2.at[step]]
        if step:
            mine = sent.at[12 + step]
            add(mine, terms)
            send(mine, held3.at[step], s3.at[step], r3.at[step], at.device(step=step))
        else:
            for other in (1, 3, 2):
                arrived(held3.at[other], r3.at[other])
                terms.append(held3.at[other])
            add(out, terms)

    order = (2, 1, 3, 0)
    for step in order:
        for second in (1, 0):
            for first in (1, 0):
                place = slot(first, second, step)
                send(
                    rows_of(share, at.block(first, second, step, sibling=1)),
                    held0.at[place],
                    s0.at[place],
                    r0.at[place],
                    at.device(sibling=1),
                )
    for turn in range(6):
        if turn < 4:
            stage_a(order[turn])
        if 1 <= turn < 5:
            stage_b(order[turn - 1])
        if 2 <= turn:
            stage_c(order[turn - 2])
    for copy in started:
        copy.wait_send()


def scatter_rows(share):
    width = share.shape[1]
    held = lambda count: pltpu.VMEM((count, 32, width), share.dtype)
    dma = pltpu.SemaphoreType.DMA
    whole = pl.BlockSpec(memory_space=pltpu.VMEM)
    return pl.pallas_call(
        scatter_kernel,
        out_shape=jax.ShapeDtypeStruct((32, width), share.dtype),
        in_specs=[whole],
        out_specs=whole,
        scratch_shapes=[held(16), held(8), held(4), held(4), held(16)]
        + [dma((count,)) for count in (16, 8, 4, 4) * 2],
        compiler_params=pltpu.CompilerParams(
            collective_id=1, has_side_effects=True, vmem_limit_bytes=40 * 1024 * 1024
        ),
        name="scatter_rows",
    )(share)


def on_device(tokens, out_grad, routes, probs, w_gate, w_up, w_down):
    n_data = lax.axis_size("dp")
    n_owner = lax.axis_size("expert")
    tok_count, top_count = routes.shape
    width = tokens.shape[1]
    routed = tok_count * top_count * n_data
    here = lax.axis_index("dp")
    expert = lax.axis_index("expert")
    torus = n_data == 2 and n_owner == 16 and tok_count == 32
    ids = jnp.arange(128 if torus else n_owner, dtype=jnp.int32)
    table = jnp.sum(
        jnp.where(routes[:, :, None] == ids, probs.astype(jnp.float32)[:, :, None], 0.0), axis=1
    ).astype(jnp.bfloat16)
    all_g = lax.all_gather(out_grad, AXES, axis=0, tiled=True)
    if torus:
        all_table, all_x = gather_rows(table, tokens)
    else:
        all_table = lax.all_gather(table, AXES, axis=0, tiled=True)
        all_x = lax.all_gather(tokens, AXES, axis=0, tiled=True)
    weight = jnp.sum(
        jnp.where(ids[None, :] == expert, all_table.astype(jnp.float32), 0.0), axis=1
    )
    capacity = min(tok_count, (tok_count * top_count * 9 + 8 * n_owner - 1) // (8 * n_owner))
    total_rows = n_data * n_owner * capacity
    flags = (weight > 0).reshape(n_data * n_owner, tok_count)
    earlier = jnp.arange(tok_count)[:, None] < jnp.arange(tok_count)[None, :]
    slot = jnp.dot(
        flags.astype(jnp.bfloat16),
        earlier.astype(jnp.bfloat16),
        preferred_element_type=jnp.float32,
    ).astype(jnp.int32)
    base = capacity * jnp.arange(n_data * n_owner, dtype=jnp.int32)
    place = jnp.where(flags, base[:, None] + slot, -1).reshape(1, -1)
    matches = place == jnp.arange(total_rows, dtype=jnp.int32)[:, None]
    chosen = matches.astype(jnp.bfloat16)
    weighted = jnp.where(matches, weight[None, :], 0.0).astype(jnp.bfloat16)
    gate = jnp.dot(all_x, w_gate[0], preferred_element_type=jnp.float32)
    upward = jnp.dot(all_x, w_up[0], preferred_element_type=jnp.float32)
    hidden = (jax.nn.silu(gate) * upward).astype(jnp.bfloat16)
    packed = jnp.dot(chosen, hidden, preferred_element_type=jnp.float32).astype(jnp.bfloat16)
    if torus:
        other = lax.ppermute(packed, "dp", [(0, 1), (1, 0)])
        both = jnp.concatenate(
            [jnp.where(here == 0, packed, other), jnp.where(here == 0, other, packed)], axis=1
        )
    else:
        both = lax.all_gather(packed, "dp", axis=1, tiled=True)
    share = weight[:, None] * jnp.dot(hidden, w_down[0], preferred_element_type=jnp.float32)
    share = share.astype(jnp.bfloat16)
    if torus:
        mixed = scatter_rows(share)
    else:
        mixed = lax.psum_scatter(share, AXES, scatter_dimension=0, tiled=True)
    input_factor = (gram(packed, both) / routed)[None]
    grad_rows = jnp.dot(weighted, all_g, preferred_element_type=jnp.float32).astype(jnp.bfloat16)
    slice_width = width // n_data
    own_cols = lax.dynamic_slice_in_dim(grad_rows, here * slice_width, slice_width, 1)
    output_factor = (gram(own_cols, grad_rows) / routed).astype(jnp.bfloat16)[None]
    return (mixed, input_factor, output_factor)


def solution(mesh):
    rows = P(AXES, None)
    in_specs = (
        rows,
        rows,
        rows,
        rows,
        P("expert", None, "dp"),
        P("expert", None, "dp"),
        P("expert", "dp", None),
    )
    out_specs = (rows, P("expert", "dp", None), P("expert", "dp", None))
    return jax.shard_map(
        on_device, mesh=mesh, in_specs=in_specs, out_specs=out_specs, check_vma=False
    )
```

```python
import jax
import jax.numpy as jnp
from jax import lax
from jax.experimental import pallas as pl
from jax.experimental.pallas import tpu as pltpu
from jax.sharding import PartitionSpec as P

AXES = ("dp", "expert")
MESH = pl.DeviceIdType.MESH
STRIP = 1024


def gram(left, right):
    return lax.dot_general(
        left, right, (((0,), (0,)), ((), ())), preferred_element_type=jnp.float32
    )


class Place:
    def __init__(self):
        self.dp = lax.axis_index("dp")
        expert = lax.axis_index("expert")
        self.z = expert // 4
        self.y = (expert // 2) % 2
        self.c = expert % 2

    def far(self, step):
        return lax.rem(self.z + step, 4)

    def flipped(self, first, second):
        over_dp = first * (1 - self.c) + second * self.c
        over_y = first * self.c + second * (1 - self.c)
        return (
            self.dp + over_dp * (1 - 2 * self.dp),
            self.y + over_y * (1 - 2 * self.y),
        )

    def device(self, first=0, second=0, step=0, sibling=0):
        dp, y = self.flipped(first, second)
        return (dp, self.far(step) * 4 + y * 2 + self.core(sibling))

    def core(self, sibling):
        return self.c + sibling * (1 - 2 * self.c)

    def block(self, first=0, second=0, step=0, sibling=0):
        dp, expert = self.device(first, second, step, sibling)
        return dp * 16 + expert

    def greet(self):
        barrier = pltpu.get_barrier_semaphore()
        peers = [self.device(step=step) for step in (1, 2, 3)]
        peers += [self.device(first=1), self.device(second=1), self.device(sibling=1)]
        for peer in peers:
            pl.semaphore_signal(barrier, inc=1, device_id=peer, device_id_type=MESH)
        pl.semaphore_wait(barrier, len(peers))


def rows_of(ref, block):
    return ref.at[pl.ds(pl.multiple_of(block * 32, 32), 32)]


def gather_kernel(count, *refs):
    ins, outs = refs[:count], refs[count : 2 * count]
    local_sem, z_sem, first_sem, second_sem, sibling_sem, recv_sem = refs[2 * count :]
    at = Place()
    at.greet()
    started = []

    def send(a, block, sem, peer, src=None):
        copy = pltpu.make_async_remote_copy(
            src_ref=rows_of(outs[a], block) if src is None else src,
            dst_ref=rows_of(outs[a], block),
            send_sem=sem,
            recv_sem=recv_sem.at[a, block],
            device_id=peer,
            device_id_type=MESH,
        )
        copy.start()
        started.append(copy)

    def arrived(a, block):
        pltpu.make_async_remote_copy(
            src_ref=rows_of(outs[a], block),
            dst_ref=rows_of(outs[a], block),
            send_sem=local_sem.at[a],
            recv_sem=recv_sem.at[a, block],
            device_id=at.device(sibling=1),
            device_id_type=MESH,
        ).wait_recv()

    def forward(a, first, second, step, own=False):
        block = at.block(first, second, step)
        src = None
        if own:
            src = ins[a]
        else:
            arrived(a, block)
        if not second:
            if not first:
                send(a, block, first_sem.at[a, step], at.device(first=1), src)
            send(a, block, second_sem.at[a, 4 * first + step], at.device(second=1), src)
        send(a, block, sibling_sem.at[a, 8 * first + 4 * second + step], at.device(sibling=1), src)

    for a in range(count):
        for step in (2, 1, 3):
            send(a, at.block(), z_sem.at[a, step], at.device(step=step), ins[a])
    local = []
    for a in range(count):
        forward(a, 0, 0, 0, own=True)
        local.append(pltpu.make_async_copy(ins[a], rows_of(outs[a], at.block()), local_sem.at[a]))
        local[-1].start()
    near, mid, far = ([], [], [])
    for step in (0, 1, 3, 2):
        if step:
            near.append((0, 0, step))
        mid.append((1, 0, step))
        far += [(0, 1, step), (1, 1, step)]
    for turn in range(count + 2):
        for a in range(count):
            stage = turn - a
            for hop in (near, mid, far)[stage] if 0 <= stage < 3 else ():
                forward(a, *hop)
    for copy in local:
        copy.wait()
    for copy in started:
        copy.wait_send()
    for a in range(count):
        for first in range(2):
            for second in range(2):
                for step in range(4):
                    arrived(a, at.block(first, second, step, sibling=1))


def gather_rows(*arrays):
    count = len(arrays)
    anywhere = pl.BlockSpec(memory_space=pl.ANY)
    dma = pltpu.SemaphoreType.DMA
    return pl.pallas_call(
        lambda *refs: gather_kernel(count, *refs),
        out_shape=[
            jax.ShapeDtypeStruct((32 * array.shape[0], array.shape[1]), array.dtype)
            for array in arrays
        ],
        in_specs=[anywhere] * count,
        out_specs=[anywhere] * count,
        scratch_shapes=[
            dma((count,)),
            dma((count, 4)),
            dma((count, 4)),
            dma((count, 8)),
            dma((count, 16)),
            dma((count, 32)),
        ],
        compiler_params=pltpu.CompilerParams(collective_id=0, has_side_effects=True),
        name="gather_rows",
    )(*arrays)


def scatter_kernel(share, out, held0, held1, held2, held3, sent, s0, s1, s2, s3, r0, r1, r2, r3):
    at = Place()
    at.greet()
    started = []

    def copy_of(src, dst, send_sem, recv_sem, peer):
        return pltpu.make_async_remote_copy(
            src_ref=src,
            dst_ref=dst,
            send_sem=send_sem,
            recv_sem=recv_sem,
            device_id=peer,
            device_id_type=MESH,
        )

    def send(*args):
        copy = copy_of(*args)
        copy.start()
        started.append(copy)

    def arrived(dst, recv_sem):
        copy_of(dst, dst, s0.at[0], recv_sem, at.device(sibling=1)).wait_recv()

    def slot(first, second, step):
        dp, y = at.flipped(first, second)
        return dp * 8 + at.far(step) * 2 + y

    def add(dst, terms):
        def strip(i, carry):
            columns = pl.ds(pl.multiple_of(i * STRIP, STRIP), STRIP)
            total = terms[0][:, columns].astype(jnp.float32)
            for term in terms[1:]:
                total = total + term[:, columns].astype(jnp.float32)
            dst[:, columns] = total.astype(dst.dtype)
            return carry

        lax.fori_loop(0, out.shape[1] // STRIP, strip, 0)

    def both_cores(first, second, step):
        place = slot(first, second, step)
        arrived(held0.at[place], r0.at[place])
        return [rows_of(share, at.block(first, second, step)), held0.at[place]]

    def stage_a(step):
        for first in range(2):
            mine = sent.at[4 * first + step]
            add(mine, both_cores(first, 1, step))
            place = 4 * first + step
            send(mine, held1.at[place], s1.at[place], r1.at[place], at.device(second=1))

    def stage_b(step):
        mine = sent.at[8 + step]
        arrived(held1.at[4 + step], r1.at[4 + step])
        add(mine, both_cores(1, 0, step) + [held1.at[4 + step]])
        send(mine, held2.at[step], s2.at[step], r2.at[step], at.device(first=1))

    def stage_c(step):
        arrived(held1.at[step], r1.at[step])
        arrived(held2.at[step], r2.at[step])
        terms = both_cores(0, 0, step) + [held1.at[step], held2.at[step]]
        if step:
            mine = sent.at[12 + step]
            add(mine, terms)
            send(mine, held3.at[step], s3.at[step], r3.at[step], at.device(step=step))
        else:
            for other in (1, 3, 2):
                arrived(held3.at[other], r3.at[other])
                terms.append(held3.at[other])
            add(out, terms)

    order = (2, 1, 3, 0)
    for step in order:
        for first in (1, 0):
            for second in (1, 0):
                place = slot(first, second, step)
                send(
                    rows_of(share, at.block(first, second, step, sibling=1)),
                    held0.at[place],
                    s0.at[place],
                    r0.at[place],
                    at.device(sibling=1),
                )
    for turn in range(6):
        if turn < 4:
            stage_a(order[turn])
        if 1 <= turn < 5:
            stage_b(order[turn - 1])
        if 2 <= turn:
            stage_c(order[turn - 2])
    for copy in started:
        copy.wait_send()


def scatter_rows(share):
    width = share.shape[1]
    held = lambda count: pltpu.VMEM((count, 32, width), share.dtype)
    dma = pltpu.SemaphoreType.DMA
    whole = pl.BlockSpec(memory_space=pltpu.VMEM)
    return pl.pallas_call(
        scatter_kernel,
        out_shape=jax.ShapeDtypeStruct((32, width), share.dtype),
        in_specs=[whole],
        out_specs=whole,
        scratch_shapes=[held(16), held(8), held(4), held(4), held(16)]
        + [dma((count,)) for count in (16, 8, 4, 4) * 2],
        compiler_params=pltpu.CompilerParams(
            collective_id=1, has_side_effects=True, vmem_limit_bytes=40 * 1024 * 1024
        ),
        name="scatter_rows",
    )(share)


def on_device(tokens, out_grad, routes, probs, w_gate, w_up, w_down):
    n_data = lax.axis_size("dp")
    n_owner = lax.axis_size("expert")
    tok_count, top_count = routes.shape
    width = tokens.shape[1]
    routed = tok_count * top_count * n_data
    here = lax.axis_index("dp")
    expert = lax.axis_index("expert")
    torus = n_data == 2 and n_owner == 16 and tok_count == 32
    ids = jnp.arange(128 if torus else n_owner, dtype=jnp.int32)
    table = jnp.sum(
        jnp.where(routes[:, :, None] == ids, probs.astype(jnp.float32)[:, :, None], 0.0), axis=1
    ).astype(jnp.bfloat16)
    all_g = lax.all_gather(out_grad, AXES, axis=0, tiled=True)
    if torus:
        all_table, all_x = gather_rows(table, tokens)
    else:
        all_table = lax.all_gather(table, AXES, axis=0, tiled=True)
        all_x = lax.all_gather(tokens, AXES, axis=0, tiled=True)
    weight = jnp.sum(
        jnp.where(ids[None, :] == expert, all_table.astype(jnp.float32), 0.0), axis=1
    )
    capacity = min(tok_count, (tok_count * top_count * 9 + 8 * n_owner - 1) // (8 * n_owner))
    total_rows = n_data * n_owner * capacity
    flags = (weight > 0).reshape(n_data * n_owner, tok_count)
    earlier = jnp.arange(tok_count)[:, None] < jnp.arange(tok_count)[None, :]
    slot = jnp.dot(
        flags.astype(jnp.bfloat16),
        earlier.astype(jnp.bfloat16),
        preferred_element_type=jnp.float32,
    ).astype(jnp.int32)
    base = capacity * jnp.arange(n_data * n_owner, dtype=jnp.int32)
    place = jnp.where(flags, base[:, None] + slot, -1).reshape(1, -1)
    matches = place == jnp.arange(total_rows, dtype=jnp.int32)[:, None]
    chosen = matches.astype(jnp.bfloat16)
    weighted = jnp.where(matches, weight[None, :], 0.0).astype(jnp.bfloat16)
    gate = jnp.dot(all_x, w_gate[0], preferred_element_type=jnp.float32)
    upward = jnp.dot(all_x, w_up[0], preferred_element_type=jnp.float32)
    hidden = (jax.nn.silu(gate) * upward).astype(jnp.bfloat16)
    packed = jnp.dot(chosen, hidden, preferred_element_type=jnp.float32).astype(jnp.bfloat16)
    if torus:
        other = lax.ppermute(packed, "dp", [(0, 1), (1, 0)])
        both = jnp.concatenate(
            [jnp.where(here == 0, packed, other), jnp.where(here == 0, other, packed)], axis=1
        )
    else:
        both = lax.all_gather(packed, "dp", axis=1, tiled=True)
    share = weight[:, None] * jnp.dot(hidden, w_down[0], preferred_element_type=jnp.float32)
    share = share.astype(jnp.bfloat16)
    if torus:
        mixed = scatter_rows(share)
    else:
        mixed = lax.psum_scatter(share, AXES, scatter_dimension=0, tiled=True)
    input_factor = (gram(packed, both) / routed)[None]
    grad_rows = jnp.dot(weighted, all_g, preferred_element_type=jnp.float32).astype(jnp.bfloat16)
    slice_width = width // n_data
    own_cols = lax.dynamic_slice_in_dim(grad_rows, here * slice_width, slice_width, 1)
    output_factor = (gram(own_cols, grad_rows) / routed).astype(jnp.bfloat16)[None]
    return (mixed, input_factor, output_factor)


def solution(mesh):
    rows = P(AXES, None)
    in_specs = (
        rows,
        rows,
        rows,
        rows,
        P("expert", None, "dp"),
        P("expert", None, "dp"),
        P("expert", "dp", None),
    )
    out_specs = (rows, P("expert", "dp", None), P("expert", "dp", None))
    return jax.shard_map(
        on_device, mesh=mesh, in_specs=in_specs, out_specs=out_specs, check_vma=False
    )
```
